1024 devices in a mesh: ctx: 256 (over z, y, x_lo), fsdp: 4 (over x_hi, core).
Axes of the slice: x: 4 (x_hi: 2, x_lo: 2; x = x_hi * 2 + x_lo), y: 8, z: 16, core: 2. Of those that a mesh axis runs over, the one named last changes fastest.
Arguments:
- features: bfloat16 [3, 32768, 6144], P(None, 'ctx', 'fsdp'), may hold values from -6 to 6
- cotangent: bfloat16 [32768, 6144], P('ctx', 'fsdp'), may hold values from -6 to 6
- master_filters: float32 [4, 7, 384], P(None, None, 'fsdp'), may hold values from -2 to 2
Outputs:
- mixed: bfloat16 [32768, 6144], P('ctx', 'fsdp')
- feature_grads: bfloat16 [3, 32768, 6144], P(None, 'ctx', 'fsdp')
- filter_grads: float32 [4, 7, 384], P(None, None, 'fsdp')
The draws below stay inside these ranges and needn't reach their ends.
All inputs are finite; a program needn't handle non-finite values.
Results may differ from the reference program's by a relative error of at most 0.007.
Values may be sent and summed in bfloat16 or wider, within the bound.
A program may use at most 32 MiB of HBM per device.

```python
import math
import jax
import jax.numpy as jnp
from jax import lax

C = 6144
G = 384
TAPS = 7
L = 32768


def block_levels(stream_key, dims, split, low, largest):
    def one(dim, parts):
        draws = jax.random.uniform(jax.random.fold_in(jax.random.fold_in(stream_key, 6), dim), (parts,), jnp.float32, low / len(split), largest / len(split))
        return jnp.repeat(jnp.exp(draws), dims[dim] // parts).reshape((-1,) + (1,) * (len(dims) - dim - 1))

    loudness = one(*split[0])
    for cut in split[1:]:
        loudness = loudness * one(*cut)
    return loudness


def bell_draw(key, extent, deviation, most, split=(), kind=jnp.bfloat16):
    level = block_levels(key, extent, split, -0.22, 0.18) if split else 1.0
    values = jax.random.normal(key, extent, jnp.float32) * deviation * level
    return jnp.minimum(jnp.maximum(values, -most), most).astype(kind)


def setup_inputs(seed: int = 0) -> dict:
    arg_keys = jax.random.split(jax.random.key(seed), 4)
    return {
        "features": bell_draw(arg_keys[0], (3, L, C), 1.0, 6.0, ((1, 256), (2, 4))),
        "cotangent": bell_draw(arg_keys[1], (L, C), 1.0, 6.0, ((0, 256), (1, 4))),
        "master_filters": bell_draw(arg_keys[2], (4, TAPS, G), TAPS ** -0.5, 2.0, ((2, 4),), jnp.float32),
    }


def causal(extended, weights):
    reach = weights.shape[0] - 1
    length = extended.shape[0] - reach
    result = weights[0] * extended[reach:reach + length]
    for lag in range(1, weights.shape[0]):
        result = result + weights[lag] * extended[reach - lag:reach - lag + length]
    return result

def anticausal(extended, weights):
    reach = weights.shape[0] - 1
    length = extended.shape[0] - reach
    result = weights[0] * extended[0:length]
    for lag in range(1, weights.shape[0]):
        result = result + weights[lag] * extended[lag:lag + length]
    return result

def reference(features, cotangent, master_filters):
    length = features.shape[1]
    channels = features.shape[2]
    groups = master_filters.shape[2]
    reach = master_filters.shape[1] - 1
    repeats = channels // groups
    rounded = master_filters.astype(jnp.bfloat16).astype(jnp.float32)
    weights = jnp.tile(rounded, (1, 1, repeats))
    width = math.gcd(channels, 512)
    count = channels // width

    def front(values):
        return jnp.pad(values, ((reach, 0), (0, 0)))

    def back(values):
        return jnp.pad(values, ((0, reach), (0, 0)))

    def one_slab(offset):
        inputs = lax.dynamic_slice_in_dim(features, offset, width, 2).astype(jnp.float32)
        upstream = lax.dynamic_slice_in_dim(cotangent, offset, width, 1).astype(jnp.float32)
        local_w = lax.dynamic_slice_in_dim(weights, offset, width, 2)
        padded = [front(inputs[i]) for i in range(3)]
        q_conv = causal(padded[0], local_w[0])
        k_conv = causal(padded[1], local_w[1])
        v_conv = causal(padded[2], local_w[2])
        product = k_conv * v_conv
        product_pad = front(product)
        mixer = causal(product_pad, local_w[3])
        mixed = (q_conv * mixer).astype(jnp.bfloat16)
        grad_qconv = upstream * mixer
        grad_mixer = upstream * q_conv
        grad_product = anticausal(back(grad_mixer), local_w[3])
        grad_kconv = grad_product * v_conv
        grad_vconv = grad_product * k_conv
        grad_q = anticausal(back(grad_qconv), local_w[0])
        grad_k = anticausal(back(grad_kconv), local_w[1])
        grad_v = anticausal(back(grad_vconv), local_w[2])
        feature_grads = jnp.stack([grad_q, grad_k, grad_v]).astype(jnp.bfloat16)
        pairs = ((grad_qconv, padded[0]), (grad_kconv, padded[1]), (grad_vconv, padded[2]), (grad_mixer, product_pad))
        rows_out = []
        for grad_term, source in pairs:
            rows_out.append(jnp.stack([lax.optimization_barrier(jnp.sum(grad_term * source[reach - lag:reach - lag + length], axis=0)) for lag in range(reach + 1)]))
        return (mixed, feature_grads, jnp.stack(rows_out))
    offsets = (jnp.arange(count) * width).astype(jnp.int32)
    mixed_b, grads_b, filt_b = lax.map(one_slab, offsets)
    mixed = jnp.transpose(mixed_b, (1, 0, 2)).reshape(length, channels)
    feature_grads = jnp.transpose(grads_b, (1, 2, 0, 3)).reshape(3, length, channels)
    per_channel = jnp.transpose(filt_b, (1, 2, 0, 3)).reshape(4, reach + 1, channels)
    summed = lax.optimization_barrier(jnp.sum(per_channel.reshape(4, reach + 1, repeats, groups), axis=2))
    factor = 1.0 / math.sqrt(length * repeats)
    return (mixed, feature_grads, summed * factor)
```

```python
import functools
import math

import jax
import jax.numpy as jnp
from jax import lax
from jax.experimental import pallas as pl
from jax.experimental.pallas import tpu as pltpu
from jax.sharding import PartitionSpec as P

LO = 2
NY = 8
TAPS = 7
LANE = 128
F32 = jnp.float32
BF16 = jnp.bfloat16


def chunks(total, most=64):
    return [(at, min(most, total - at)) for at in range(0, total, most)]


def kernel(
    n_ctx, n_f, ny, factor,
    feat, cot, mast,
    mixed_o, grads_o, filt_o,
    hl_q, hl_kv, hr_c, hr_q, hr_kv, wg, wv,
    xq, xk, xv, xc, qc, kc, vc, pr, gm, gq, gk, gv, acc,
    s1s, s1r, s2s, s2r, s3s, s3r, res,
    halo_ss, halo_rs, filt_ss, filt_rs,
    s1_ss, s1_rs, s2_ss, s2_rs, s3_ss, s3_rs, s4_ss, s4_rs,
):
    length = feat.shape[1]
    blocks = feat.shape[2] // LANE
    portion = mast.shape[2]
    nz = n_ctx // (LO * ny)
    nx = n_f * LO
    ctx = lax.axis_index("ctx")
    f = lax.axis_index("fsdp")
    lo = lax.rem(ctx, LO)
    y = lax.rem(lax.div(ctx, LO), ny)
    z = lax.div(ctx, LO * ny)
    x8 = f * LO + lo

    def dev(z_, y_, lo_, f_):
        return ((z_ * ny + y_) * LO + lo_, f_)

    def row_dev(s):
        return dev(z, y, lax.rem(s, LO), lax.div(s, LO))

    nxt = (lax.rem(ctx + 1, n_ctx), f)
    prv = (lax.rem(ctx + n_ctx - 1, n_ctx), f)

    def remote(src, dst, ss, rs, device):
        return pltpu.make_async_remote_copy(
            src_ref=src, dst_ref=dst, send_sem=ss, recv_sem=rs,
            device_id=device, device_id_type=pl.DeviceIdType.MESH,
        )

    partners = [row_dev(lax.rem(x8 + d, nx)) for d in range(1, nx)]
    partners += [dev(z, lax.rem(y + d, ny), lo, f) for d in range(1, ny)]
    partners += [dev(lax.rem(z + d, nz), y, lo, f) for d in range(1, nz)]
    partners += [
        dev(z, lax.rem(y + d + ny, ny), 1 - lo, f) for d in (-2, -1, 1, 2)
    ]
    partners += [nxt, prv]
    barrier = pltpu.get_barrier_semaphore()
    for device in partners:
        pl.semaphore_signal(
            barrier, inc=1, device_id=device, device_id_type=pl.DeviceIdType.MESH
        )
    acc[...] = jnp.zeros_like(acc)
    wg[f] = mast[...]
    pl.semaphore_wait(barrier, len(partners))

    filt = []
    for d in range(1, n_f):
        copy = remote(
            mast, wg.at[f], filt_ss.at[d], filt_rs.at[f],
            (ctx, lax.rem(f + d, n_f)),
        )
        copy.start()
        filt.append(copy)
    halo_plan = [
        (feat.at[pl.ds(1, 2), pl.ds(length - 16, 16), :], hl_kv, nxt),
        (feat.at[0, pl.ds(length - 8, 8), :], hl_q, nxt),
        (cot.at[pl.ds(0, 16), :], hr_c, prv),
        (feat.at[0, pl.ds(0, 16), :], hr_q, prv),
        (feat.at[pl.ds(1, 2), pl.ds(0, 8), :], hr_kv, prv),
    ]
    halo = []
    for i, (src, dst, device) in enumerate(halo_plan):
        copy = remote(src, dst, halo_ss.at[i], halo_rs.at[i], device)
        copy.start()
        halo.append(copy)

    for d in range(1, n_f):
        src = lax.rem(f + d, n_f)
        remote(mast, wg.at[src], filt_ss.at[d], filt_rs.at[src], (ctx, src)).wait_recv()
    for j in range(TAPS):
        whole = jnp.concatenate([wg[i, j] for i in range(n_f)], axis=1)
        whole = whole.astype(BF16).astype(F32)
        for m in range(whole.shape[1] // LANE):
            wv[m, j] = whole[:, m * LANE : (m + 1) * LANE]
    for copy in halo:
        copy.wait_recv()

    tiles = wv.shape[0]
    first = ctx == 0
    last = ctx == n_ctx - 1

    def taps(m, bank):
        return [wv[m, j, pl.ds(bank, 1), :] for j in range(TAPS)]

    def fir(ref, at, rows, w, sign):
        total = w[0] * ref[pl.ds(at, rows), :]
        for j in range(1, TAPS):
            total = total + w[j] * ref[pl.ds(at + sign * j, rows), :]
        return total

    def first_pass(b, carry):
        m = lax.rem(b, tiles)
        lanes = pl.ds(pl.multiple_of(b * LANE, LANE), LANE)

        def edge(ref, drop):
            return jnp.where(drop, 0.0, ref[:, lanes].astype(F32))

        for ref, i in ((xq, 0), (xk, 1), (xv, 2)):
            ref[16 : 16 + length, :] = feat[i, :, lanes].astype(F32)
        xc[0:length, :] = cot[:, lanes].astype(F32)
        xq[8:16, :] = edge(hl_q, first)
        xk[0:16, :] = edge(hl_kv.at[0], first)
        xv[0:16, :] = edge(hl_kv.at[1], first)
        xc[length : length + 16, :] = edge(hr_c, last)
        xq[16 + length : 32 + length, :] = edge(hr_q, last)
        xk[16 + length : 24 + length, :] = edge(hr_kv.at[0], last)
        xv[16 + length : 24 + length, :] = edge(hr_kv.at[1], last)

        w = taps(m, 0)
        for at, rows in chunks(length + 16):
            conv = fir(xq, 16 + at, rows, w, -1)
            qc[at : at + rows, :] = conv
            gm[at : at + rows, :] = conv * xc[at : at + rows, :]
        w = taps(m, 1)
        for at, rows in chunks(length + 16):
            kc[at : at + rows, :] = fir(xk, 8 + at, rows, w, -1)
        w = taps(m, 2)
        for at, rows in chunks(length + 16):
            conv = fir(xv, 8 + at, rows, w, -1)
            vc[at : at + rows, :] = conv
            pr[at : at + rows, :] = conv * kc[at : at + rows, :]
        w = taps(m, 3)
        for at, rows in chunks(length + 8):
            mixer = fir(pr, 8 + at, rows, w, -1)
            gq[b, at : at + rows, :] = mixer * xc[at : at + rows, :]
            kept = min(rows, length - at)
            if kept > 0:
                mixed_o[at : at + kept, lanes] = (
                    mixer[:kept] * qc[at : at + kept, :]
                ).astype(BF16)
        for at, rows in chunks(length + 8):
            grad = fir(gm, at, rows, w, 1)
            gk[b, at : at + rows, :] = grad * vc[8 + at : 8 + at + rows, :]
            gv[b, at : at + rows, :] = grad * kc[8 + at : 8 + at + rows, :]

        for bank, (grad, source, off) in enumerate(
            ((gq.at[b], xq, 16), (gk.at[b], xk, 16), (gv.at[b], xv, 16), (gm, pr, 8))
        ):
            sums = [None] * TAPS
            for at, rows in chunks(length):
                g = grad[at : at + rows, :]
                for j in range(TAPS):
                    part = g * source[pl.ds(off + at - j, rows), :]
                    part = jnp.sum(part.reshape(rows // 8, 8, LANE), axis=0)
                    sums[j] = part if sums[j] is None else sums[j] + part
            for j in range(TAPS):
                acc[m, 4 * j + bank] = acc[m, 4 * j + bank] + sums[j]
        return carry

    lax.fori_loop(0, blocks, first_pass, 0)

    lane_at = lax.broadcasted_iota(jnp.int32, (8, LANE), 1)
    for pair in range(4):
        parts = [
            jnp.sum(acc[m, 8 * pair : 8 * pair + 8], axis=1) for m in range(tiles)
        ]
        for g in range(n_f):
            m, off = divmod(g * portion, LANE)
            piece = pltpu.roll(parts[m], (LANE - off) % LANE, 1) if off else parts[m]
            if off + portion > LANE:
                rest = pltpu.roll(parts[m + 1], LANE - off, 1)
                piece = jnp.where(lane_at < LANE - off, piece, rest)
            for i in range(2):
                half, tap = divmod(2 * pair + i, 4)
                s1s[g * LO + half, tap] = piece[4 * i : 4 * i + 4]
    sends = []
    for d in range(1, nx):
        s = lax.rem(x8 + d, nx)
        copy = remote(s1s.at[s], s1r.at[x8], s1_ss.at[d], s1_rs.at[x8], row_dev(s))
        copy.start()
        sends.append(copy)
    s1r[x8] = s1s[x8]
    for d in range(1, nx):
        s = lax.rem(x8 + d, nx)
        remote(s1s.at[s], s1r.at[s], s1_ss.at[d], s1_rs.at[s], row_dev(s)).wait_recv()
    total = s1r[0]
    for s in range(1, nx):
        total = total + s1r[s]
    s2s[...] = total

    mine = lax.rem(y, 4)
    for d in range(1, ny):
        s = lax.rem(y + d, ny)
        copy = remote(
            s2s.at[lax.rem(s, 4)], s2r.at[y], s2_ss.at[d], s2_rs.at[y], dev(z, s, lo, f)
        )
        copy.start()
        sends.append(copy)
    s2r[y] = s2s[mine]
    for d in range(1, ny):
        s = lax.rem(y + d, ny)
        remote(
            s2s.at[mine], s2r.at[s], s2_ss.at[d], s2_rs.at[s], dev(z, s, lo, f)
        ).wait_recv()
    total = s2r[0]
    for s in range(1, ny):
        total = total + s2r[s]
    s3s[...] = total

    for d in range(1, nz):
        s = lax.rem(z + d, nz)
        copy = remote(s3s, s3r.at[z], s3_ss.at[d], s3_rs.at[z], dev(s, y, lo, f))
        copy.start()
        sends.append(copy)
    s3r[z] = s3s[...]

    def second_pass(b, carry):
        m = lax.rem(b, tiles)
        lanes = pl.ds(pl.multiple_of(b * LANE, LANE), LANE)
        for bank, grad in enumerate((gq.at[b], gk.at[b], gv.at[b])):
            w = taps(m, bank)
            for at, rows in chunks(length):
                grads_o[bank, at : at + rows, lanes] = fir(grad, at, rows, w, 1).astype(BF16)
        return carry

    lax.fori_loop(0, blocks, second_pass, 0)

    for d in range(1, nz):
        s = lax.rem(z + d, nz)
        remote(s3s, s3r.at[s], s3_ss.at[d], s3_rs.at[s], dev(s, y, lo, f)).wait_recv()
    total = s3r[0]
    for s in range(1, nz):
        total = total + s3r[s]
    res[lo * 4 + mine] = total

    piece = res.at[lo * 4 + mine]
    n_send = 0
    for d in (0, -1, 1, 2):
        for other in (0, 1):
            if d == 0 and other == 0:
                continue
            lo_ = 1 - lo if other else lo
            copy = remote(
                piece, piece, s4_ss.at[n_send], s4_rs.at[lo * 4 + mine],
                dev(z, lax.rem(y + d + ny, ny), lo_, f),
            )
            copy.start()
            sends.append(copy)
            n_send += 1
    for d in range(1, LO * 4):
        s = lax.rem(lo * 4 + mine + d, LO * 4)
        remote(piece, res.at[s], s4_ss.at[0], s4_rs.at[s], nxt).wait_recv()
    for j in range(TAPS):
        filt_o[j] = res[j][:, :portion] * factor

    for copy in filt + halo + sends:
        copy.wait_send()


def per_device(n_ctx, n_f, ny, features, cotangent, master_filters):
    _, length, width = features.shape
    portion = master_filters.shape[2]
    groups = portion * n_f
    repeats = width // groups
    count_all = length * n_ctx * repeats * n_f
    factor = 1.0 / math.sqrt(count_all)
    nz = n_ctx // (LO * ny)
    nx = n_f * LO
    blocks = width // LANE
    tiles = groups // LANE
    vm = pltpu.VMEM
    dma = pltpu.SemaphoreType.DMA
    scratch = [
        vm((8, width), BF16), vm((2, 16, width), BF16),
        vm((16, width), BF16), vm((16, width), BF16), vm((2, 8, width), BF16),
        vm((n_f, TAPS, 4, portion), F32), vm((tiles, TAPS, 4, LANE), F32),
    ]
    scratch += [vm((length + 32, LANE), F32)] * 3 + [vm((length + 16, LANE), F32)] * 6
    scratch += [vm((blocks, length + 8, LANE), F32)] * 3
    scratch += [
        vm((tiles, 32, 8, LANE), F32),
        vm((nx, 4, 4, LANE), F32), vm((nx, 4, 4, LANE), F32),
        vm((4, 4, LANE), F32), vm((ny, 4, LANE), F32),
        vm((4, LANE), F32), vm((nz, 4, LANE), F32), vm((8, 4, LANE), F32),
        dma((5,)), dma((5,)), dma((n_f,)), dma((n_f,)),
        dma((nx,)), dma((nx,)), dma((ny,)), dma((ny,)), dma((nz,)), dma((nz,)),
        dma((7,)), dma((8,)),
    ]
    vmem = pl.BlockSpec(memory_space=pltpu.MemorySpace.VMEM)
    mixed, grads, filters = pl.pallas_call(
        functools.partial(kernel, n_ctx, n_f, ny, factor),
        out_shape=(
            jax.ShapeDtypeStruct((length, width), BF16),
            jax.ShapeDtypeStruct((3, length, width), BF16),
            jax.ShapeDtypeStruct((TAPS, 4, portion), F32),
        ),
        in_specs=[vmem] * 3,
        out_specs=(vmem, vmem, vmem),
        scratch_shapes=scratch,
        compiler_params=pltpu.CompilerParams(
            collective_id=0, has_side_effects=True, vmem_limit_bytes=40 * 1024 * 1024
        ),
    )(features, cotangent, jnp.transpose(master_filters, (1, 0, 2)))
    return mixed, grads, jnp.transpose(filters, (1, 0, 2))


def solution(mesh, ny=NY):
    return jax.shard_map(
        functools.partial(per_device, mesh.shape["ctx"], mesh.shape["fsdp"], ny),
        mesh=mesh,
        in_specs=(P(None, "ctx", "fsdp"), P("ctx", "fsdp"), P(None, None, "fsdp")),
        out_specs=(P("ctx", "fsdp"), P(None, "ctx", "fsdp"), P(None, None, "fsdp")),
        check_vma=False,
    )
```

```python
import functools
import math

import jax
import jax.numpy as jnp
from jax import lax
from jax.experimental import pallas as pl
from jax.experimental.pallas import tpu as pltpu
from jax.sharding import PartitionSpec as P

LO = 2
NY = 8
TAPS = 7
LANE = 128
F32 = jnp.float32
BF16 = jnp.bfloat16
ALL_VMEM = 67043328


def chunks(first, end, most=64):
    return [(at, min(most, end - at)) for at in range(first, end, most)]


def far_first(n):
    return sorted(range(1, n), key=lambda d: -min(d, n - d))


def kernel(
    n_ctx, n_f, ny,
    feat, cot, mast,
    mixed_o, grads_o, res,
    fb, cb, mb, gb, hl_q, hl_kv, hr_c, hr_q, lr_c, lr_q, lr_kv, wg, wv,
    xq, xk, xv, xc, qc, kc, vc, pr, gm, gq, gk, gv, acc,
    s1s, s1r, s2s, s2r, s3s, s3r, s4s,
    load_sem, halo_ss, halo_rs, filt_ss, filt_rs,
    s1_ss, s1_rs, s2_ss, s2_rs, s3_ss, s3_rs, s4_ss, s4_rs, out_sem, near_sem,
):
    length = fb.shape[1]
    blocks = fb.shape[2] // LANE
    portion = mast.shape[2]
    tiles = wv.shape[0]
    nz = n_ctx // (LO * ny)
    nx = n_f * LO
    ctx = lax.axis_index("ctx")
    f = lax.axis_index("fsdp")
    lo = lax.rem(ctx, LO)
    y = lax.rem(lax.div(ctx, LO), ny)
    z = lax.div(ctx, LO * ny)
    x8 = f * LO + lo
    first = ctx == 0
    last = ctx == n_ctx - 1

    def dev(z_, y_, lo_, f_):
        return ((z_ * ny + y_) * LO + lo_, f_)

    def row_dev(s):
        return dev(z, y, lax.rem(s, LO), lax.div(s, LO))

    nxt = (lax.rem(ctx + 1, n_ctx), f)
    prv = (lax.rem(ctx + n_ctx - 1, n_ctx), f)

    def remote(src, dst, ss, rs, device):
        return pltpu.make_async_remote_copy(
            src_ref=src, dst_ref=dst, send_sem=ss, recv_sem=rs,
            device_id=device, device_id_type=pl.DeviceIdType.MESH,
        )

    def at_z(d):
        return dev(lax.rem(z + d + nz, nz), y, lo, f)

    def at_y(d):
        return dev(z, lax.rem(y + d + ny, ny), lo, f)

    partners = [nxt, prv]
    if nz > 1:
        partners += [at_z(1), at_z(-1)]
    if ny > 1:
        partners += [at_y(1), at_y(-1)]
    partners += [row_dev(lax.rem(x8 + d, nx)) for d in range(1, nx)]
    barrier = pltpu.get_barrier_semaphore()
    for device in partners:
        pl.semaphore_signal(
            barrier, inc=1, device_id=device, device_id_type=pl.DeviceIdType.MESH
        )
    loads = [
        pltpu.make_async_copy(feat, fb, load_sem.at[0]),
        pltpu.make_async_copy(cot, cb, load_sem.at[1]),
        pltpu.make_async_copy(mast, wg.at[f], load_sem.at[2]),
    ]
    for copy in loads:
        copy.start()
    acc[...] = jnp.zeros_like(acc)
    pl.semaphore_wait(barrier, len(partners))

    def tell(step):
        reach = 1 << step
        for i, (n, at) in enumerate(((nz, at_z), (ny, at_y))):
            if reach < n // 2:
                for d in (reach, -reach):
                    pl.semaphore_signal(
                        near_sem.at[step, i], inc=1, device_id=at(d),
                        device_id_type=pl.DeviceIdType.MESH,
                    )

    def hear(step):
        reach = 1 << step
        for i, n in enumerate((nz, ny)):
            if reach < n // 2:
                pl.semaphore_wait(near_sem.at[step, i], 2)

    tell(0)

    kept = []
    for d in range(1, n_f):
        copy = remote(
            mast, wg.at[f], filt_ss.at[d], filt_rs.at[f],
            (ctx, lax.rem(f + d, n_f)),
        )
        copy.start()
        kept.append(copy)
    halo_plan = [
        (feat.at[pl.ds(1, 2), pl.ds(length - 16, 16), :], hl_kv, nxt),
        (feat.at[0, pl.ds(length - 8, 8), :], hl_q, nxt),
        (cot.at[pl.ds(0, 8), :], hr_c, prv),
        (feat.at[0, pl.ds(0, 8), :], hr_q, prv),
        (cot.at[pl.ds(8, 8), :], lr_c, prv),
        (feat.at[0, pl.ds(8, 8), :], lr_q, prv),
        (feat.at[pl.ds(1, 2), pl.ds(0, 8), :], lr_kv, prv),
    ]
    halo = []
    for i, (src, dst, device) in enumerate(halo_plan):
        copy = remote(src, dst, halo_ss.at[i], halo_rs.at[i], device)
        if i < 4:
            copy.start()
        halo.append(copy)
    kept += halo

    for copy in loads:
        copy.wait()
    for d in range(1, n_f):
        src = lax.rem(f + d, n_f)
        remote(mast, wg.at[src], filt_ss.at[d], filt_rs.at[src], (ctx, src)).wait_recv()
    hear(0)
    tell(1)
    for j in range(TAPS):
        whole = jnp.concatenate([wg[i, j] for i in range(n_f)], axis=1)
        whole = whole.astype(BF16).astype(F32)
        for m in range(tiles):
            wv[m, j] = whole[:, m * LANE : (m + 1) * LANE]

    def taps(m, bank):
        return [wv[m, j, pl.ds(bank, 1), :] for j in range(TAPS)]

    def fir(ref, at, rows, w, sign):
        total = w[0] * ref[pl.ds(at, rows), :]
        for j in range(1, TAPS):
            total = total + w[j] * ref[pl.ds(at + sign * j, rows), :]
        return total

    def lanes_of(b):
        return pl.ds(pl.multiple_of(b * LANE, LANE), LANE)

    def q_rows(b, m, spans):
        w = taps(m, 0)
        for at, rows in spans:
            conv = fir(xq.at[b], 16 + at, rows, w, -1)
            qc[b, at : at + rows, :] = conv
            gm[b, at : at + rows, :] = conv * xc[b, at : at + rows, :]

    def kv_rows(b, m, spans):
        w = taps(m, 1)
        for at, rows in spans:
            kc[b, 8 + at : 8 + at + rows, :] = fir(xk.at[b], 16 + at, rows, w, -1)
        w = taps(m, 2)
        for at, rows in spans:
            own = slice(8 + at, 8 + at + rows)
            conv = fir(xv.at[b], 16 + at, rows, w, -1)
            vc[b, own, :] = conv
            pr[b, own, :] = conv * kc[b, own, :]

    def mixer_rows(b, m, spans, keep=True):
        w = taps(m, 3)
        for at, rows in spans:
            mixer = fir(pr.at[b], 8 + at, rows, w, -1)
            gq[b, at : at + rows, :] = mixer * xc[b, at : at + rows, :]
            if keep:
                mb[at : at + rows, lanes_of(b)] = (
                    mixer * qc[b, at : at + rows, :]
                ).astype(BF16)

    def product_rows(b, m, spans):
        w = taps(m, 3)
        for at, rows in spans:
            own = slice(8 + at, 8 + at + rows)
            grad = fir(gm.at[b], at, rows, w, 1)
            gk[b, at : at + rows, :] = grad * vc[b, own, :]
            gv[b, at : at + rows, :] = grad * kc[b, own, :]

    def filter_rows(b, m, bank, spans):
        grad = (gq, gk, gv, gm)[bank].at[b]
        source = (xq, xk, xv, pr)[bank].at[b]
        off = 8 if bank == 3 else 16
        sums = [None] * TAPS
        for at, rows in spans:
            g = grad[at : at + rows, :]
            for j in range(TAPS):
                part = g * source[pl.ds(off + at - j, rows), :]
                part = jnp.sum(part.reshape(rows // 8, 8, LANE), axis=0)
                sums[j] = part if sums[j] is None else sums[j] + part
        for j in range(TAPS):
            acc[m, 4 * j + bank] = acc[m, 4 * j + bank] + sums[j]

    def interior(b, carry):
        m = lax.rem(b, tiles)
        lanes = lanes_of(b)
        for ref, i in ((xq, 0), (xk, 1), (xv, 2)):
            ref[b, 16 : 16 + length, :] = fb[i, :, lanes].astype(F32)
        xc[b, 0:length, :] = cb[:, lanes].astype(F32)
        q_rows(b, m, chunks(8, length))
        kv_rows(b, m, chunks(8, length))
        mixer_rows(b, m, chunks(16, length))
        product_rows(b, m, chunks(8, length - 8))
        filter_rows(b, m, 0, chunks(16, length))
        filter_rows(b, m, 1, chunks(8, length - 8))
        filter_rows(b, m, 2, chunks(8, length - 8))
        filter_rows(b, m, 3, chunks(16, length))
        return carry

    lax.fori_loop(0, blocks, interior, 0)
    for copy in halo[4:]:
        copy.start()
    hear(1)
    tell(2)
    for copy in halo[:4]:
        copy.wait_recv()

    def edge(ref, lanes, drop):
        return jnp.where(drop, 0.0, ref[:, lanes].astype(F32))

    def edges(b, carry):
        m = lax.rem(b, tiles)
        lanes = lanes_of(b)
        xq[b, 8:16, :] = edge(hl_q, lanes, first)
        xk[b, 0:16, :] = edge(hl_kv.at[0], lanes, first)
        xv[b, 0:16, :] = edge(hl_kv.at[1], lanes, first)
        xc[b, length : length + 8, :] = edge(hr_c, lanes, last)
        xq[b, 16 + length : 24 + length, :] = edge(hr_q, lanes, last)
        ends = [(0, 8), (length - 8, 8)]
        q_rows(b, m, [(0, 8), (length, 8)])
        kv_rows(b, m, [(-8, 16)])
        mixer_rows(b, m, [(0, 16)])
        product_rows(b, m, ends)
        filter_rows(b, m, 0, [(0, 16)])
        filter_rows(b, m, 1, ends)
        filter_rows(b, m, 2, ends)
        filter_rows(b, m, 3, [(0, 16)])
        return carry

    lax.fori_loop(0, blocks, edges, 0)
    out_mixed = pltpu.make_async_copy(mb, mixed_o, out_sem.at[0])
    out_mixed.start()

    lane_at = lax.broadcasted_iota(jnp.int32, (8, LANE), 1)
    for pair in range(4):
        parts = [
            jnp.sum(acc[m, 8 * pair : 8 * pair + 8], axis=1) for m in range(tiles)
        ]
        for g in range(n_f):
            m, off = divmod(g * portion, LANE)
            piece = pltpu.roll(parts[m], (LANE - off) % LANE, 1) if off else parts[m]
            if off + portion > LANE:
                rest = pltpu.roll(parts[m + 1], LANE - off, 1)
                piece = jnp.where(lane_at < LANE - off, piece, rest)
            for i in range(2):
                half, tap = divmod(2 * pair + i, 4)
                s1s[g * LO + half, tap] = piece[4 * i : 4 * i + 4]
    for d in range(1, nx):
        s = lax.rem(x8 + d, nx)
        copy = remote(s1s.at[s], s1r.at[x8], s1_ss.at[d], s1_rs.at[x8], row_dev(s))
        copy.start()
        kept.append(copy)
    s1r[x8] = s1s[x8]
    for d in range(1, nx):
        s = lax.rem(x8 + d, nx)
        remote(s1s.at[s], s1r.at[s], s1_ss.at[d], s1_rs.at[s], row_dev(s)).wait_recv()
    total = s1r[0]
    for s in range(1, nx):
        total = total + s1r[s]
    s2s[...] = total

    mine = lax.rem(y, 4)
    for d in far_first(ny):
        s = lax.rem(y + d, ny)
        copy = remote(
            s2s.at[lax.rem(s, 4)], s2r.at[y], s2_ss.at[d], s2_rs.at[y], dev(z, s, lo, f)
        )
        copy.start()
        kept.append(copy)
    s2r[y] = s2s[mine]
    for d in range(1, ny):
        s = lax.rem(y + d, ny)
        remote(
            s2s.at[mine], s2r.at[s], s2_ss.at[d], s2_rs.at[s], dev(z, s, lo, f)
        ).wait_recv()
    total = s2r[0]
    for s in range(1, ny):
        total = total + s2r[s]
    s3s[...] = total

    hear(2)
    for d in far_first(nz):
        s = lax.rem(z + d, nz)
        copy = remote(s3s, s3r.at[z], s3_ss.at[d], s3_rs.at[z], dev(s, y, lo, f))
        copy.start()
        kept.append(copy)
    s3r[z] = s3s[...]

    for copy in halo[4:]:
        copy.wait_recv()

    def second_pass(b, carry):
        m = lax.rem(b, tiles)
        lanes = lanes_of(b)
        xc[b, length + 8 : length + 16, :] = edge(lr_c, lanes, last)
        xq[b, 24 + length : 32 + length, :] = edge(lr_q, lanes, last)
        xk[b, 16 + length : 24 + length, :] = edge(lr_kv.at[0], lanes, last)
        xv[b, 16 + length : 24 + length, :] = edge(lr_kv.at[1], lanes, last)
        past = [(length, 8)]
        q_rows(b, m, [(length + 8, 8)])
        kv_rows(b, m, past)
        mixer_rows(b, m, past, keep=False)
        product_rows(b, m, past)
        for bank, grad in enumerate((gq.at[b], gk.at[b], gv.at[b])):
            w = taps(m, bank)
            for at, rows in chunks(0, length):
                gb[bank, at : at + rows, lanes] = fir(grad, at, rows, w, 1).astype(BF16)
        return carry

    lax.fori_loop(0, blocks, second_pass, 0)
    out_grads = pltpu.make_async_copy(gb, grads_o, out_sem.at[1])
    out_grads.start()

    for d in range(1, nz):
        s = lax.rem(z + d, nz)
        remote(s3s, s3r.at[s], s3_ss.at[d], s3_rs.at[s], dev(s, y, lo, f)).wait_recv()
    total = s3r[0]
    for s in range(1, nz):
        total = total + s3r[s]
    s4s[...] = total

    tap = lo * 4 + mine
    for i, (d, other) in enumerate(
        ((2, 1), (2, 0), (-1, 1), (1, 1), (-1, 0), (1, 0), (0, 1))
    ):
        device = dev(z, lax.rem(y + d + ny, ny), 1 - lo if other else lo, f)
        copy = remote(s4s, res.at[tap], s4_ss.at[i], s4_rs.at[tap], device)
        copy.start()
        kept.append(copy)
    out_res = pltpu.make_async_copy(s4s, res.at[tap], out_sem.at[2])
    out_res.start()
    for d in range(1, LO * 4):
        s = lax.rem(tap + d, LO * 4)
        remote(s4s, res.at[s], s4_ss.at[0], s4_rs.at[s], nxt).wait_recv()

    for copy in kept:
        copy.wait_send()
    out_mixed.wait()
    out_grads.wait()
    out_res.wait()


def write(factor, mixed, grads, res, mixed_o, grads_o, filt_o, big, small, done, sem):
    pieces = [(res, small)] + [(mixed, big.at[3])]
    pieces += [(grads.at[i], big.at[i]) for i in range(3)]
    reads = [
        pltpu.make_async_copy(src, dst, sem.at[0, i])
        for i, (src, dst) in enumerate(pieces)
    ]
    for copy in reads:
        copy.start()
    reads[0].wait()
    portion = filt_o.shape[2]
    for j in range(TAPS):
        done[j] = small[j][:, :portion] * factor
    outs = [(done, filt_o), (big.at[3], mixed_o)]
    outs += [(big.at[i], grads_o.at[i]) for i in range(3)]
    writes = [
        pltpu.make_async_copy(src, dst, sem.at[1, i])
        for i, (src, dst) in enumerate(outs)
    ]
    writes[0].start()
    for i in range(1, 5):
        reads[i].wait()
        writes[i].start()
    for copy in writes:
        copy.wait()


def per_device(n_ctx, n_f, ny, features, cotangent, master_filters):
    _, length, width = features.shape
    portion = master_filters.shape[2]
    groups = portion * n_f
    repeats = width // groups
    count_all = length * n_ctx * repeats * n_f
    factor = 1.0 / math.sqrt(count_all)
    nz = n_ctx // (LO * ny)
    nx = n_f * LO
    blocks = width // LANE
    tiles = groups // LANE
    vm = pltpu.VMEM
    dma = pltpu.SemaphoreType.DMA
    scratch = [
        vm((3, length, width), BF16), vm((length, width), BF16),
        vm((length, width), BF16), vm((3, length, width), BF16),
        vm((8, width), BF16), vm((2, 16, width), BF16),
        vm((8, width), BF16), vm((8, width), BF16),
        vm((8, width), BF16), vm((8, width), BF16), vm((2, 8, width), BF16),
        vm((n_f, TAPS, 4, portion), F32), vm((tiles, TAPS, 4, LANE), F32),
    ]
    scratch += [vm((blocks, length + 32, LANE), F32)] * 3
    scratch += [vm((blocks, length + 16, LANE), F32)] * 6
    scratch += [vm((blocks, length + 8, LANE), F32)] * 3
    scratch += [
        vm((tiles, 32, 8, LANE), F32),
        vm((nx, 4, 4, LANE), F32), vm((nx, 4, 4, LANE), F32),
        vm((4, 4, LANE), F32), vm((ny, 4, LANE), F32),
        vm((4, LANE), F32), vm((nz, 4, LANE), F32), vm((4, LANE), F32),
        dma((3,)), dma((7,)), dma((7,)), dma((n_f,)), dma((n_f,)),
        dma((nx,)), dma((nx,)), dma((ny,)), dma((ny,)), dma((nz,)), dma((nz,)),
        dma((7,)), dma((8,)), dma((3,)), pltpu.SemaphoreType.REGULAR((3, 2)),
    ]
    anywhere = pl.BlockSpec(memory_space=pl.ANY)
    big = (
        jax.ShapeDtypeStruct((length, width), BF16),
        jax.ShapeDtypeStruct((3, length, width), BF16),
    )
    mixed, grads, res = pl.pallas_call(
        functools.partial(kernel, n_ctx, n_f, ny),
        out_shape=big + (jax.ShapeDtypeStruct((8, 4, LANE), F32),),
        in_specs=[anywhere] * 3,
        out_specs=(anywhere,) * 3,
        scratch_shapes=scratch,
        compiler_params=pltpu.CompilerParams(
            collective_id=0, has_side_effects=True, vmem_limit_bytes=ALL_VMEM
        ),
    )(features, cotangent, jnp.transpose(master_filters, (1, 0, 2)))
    mixed, grads, filters = pl.pallas_call(
        functools.partial(write, factor),
        out_shape=big + (jax.ShapeDtypeStruct((TAPS, 4, portion), F32),),
        in_specs=[anywhere] * 3,
        out_specs=(anywhere,) * 3,
        scratch_shapes=[
            vm((4, length, width), BF16), vm((8, 4, LANE), F32),
            vm((TAPS, 4, portion), F32), dma((2, 5)),
        ],
        compiler_params=pltpu.CompilerParams(vmem_limit_bytes=ALL_VMEM),
    )(mixed, grads, res)
    return mixed, grads, jnp.transpose(filters, (1, 0, 2))


def solution(mesh, ny=NY):
    return jax.shard_map(
        functools.partial(per_device, mesh.shape["ctx"], mesh.shape["fsdp"], ny),
        mesh=mesh,
        in_specs=(P(None, "ctx", "fsdp"), P("ctx", "fsdp"), P(None, None, "fsdp")),
        out_specs=(P("ctx", "fsdp"), P(None, "ctx", "fsdp"), P(None, None, "fsdp")),
        check_vma=False,
    )
```

```python
import functools
import math

import jax
import jax.numpy as jnp
from jax import lax
from jax.experimental import pallas as pl
from jax.experimental.pallas import tpu as pltpu
from jax.sharding import PartitionSpec as P

LO = 2
NY = 8
TAPS = 7
LANE = 128
F32 = jnp.float32
BF16 = jnp.bfloat16
ALL_VMEM = 67043328


def chunks(first, end, most=64):
    return [(at, min(most, end - at)) for at in range(first, end, most)]


def far_first(n):
    return sorted(range(1, n), key=lambda d: -min(d, n - d))


def kernel(
    n_ctx, n_f, ny,
    feat, cot, mast,
    mixed_o, grads_o, res,
    fb, cb, mb, gb, hl_q, hl_kv, hr_c, hr_q, lr_c, lr_q, lr_kv, wg, wv,
    xq, xk, xv, xc, qc, kc, vc, pr, gm, gq, gk, gv, acc,
    s1s, s1r, s2s, s2r, s3s, s3r, s4s,
    load_sem, halo_ss, halo_rs, filt_ss, filt_rs,
    s1_ss, s1_rs, s2_ss, s2_rs, s3_ss, s3_rs, s4_ss, s4_rs, out_sem, near_sem,
):
    length = fb.shape[1]
    blocks = fb.shape[2] // LANE
    portion = mast.shape[2]
    tiles = wv.shape[0]
    nz = n_ctx // (LO * ny)
    nx = n_f * LO
    ctx = lax.axis_index("ctx")
    f = lax.axis_index("fsdp")
    lo = lax.rem(ctx, LO)
    y = lax.rem(lax.div(ctx, LO), ny)
    z = lax.div(ctx, LO * ny)
    x8 = f * LO + lo
    first = ctx == 0
    last = ctx == n_ctx - 1

    def dev(z_, y_, lo_, f_):
        return ((z_ * ny + y_) * LO + lo_, f_)

    def row_dev(s):
        return dev(z, y, lax.rem(s, LO), lax.div(s, LO))

    nxt = (lax.rem(ctx + 1, n_ctx), f)
    prv = (lax.rem(ctx + n_ctx - 1, n_ctx), f)

    def remote(src, dst, ss, rs, device):
        return pltpu.make_async_remote_copy(
            src_ref=src, dst_ref=dst, send_sem=ss, recv_sem=rs,
            device_id=device, device_id_type=pl.DeviceIdType.MESH,
        )

    def at_z(d):
        return dev(lax.rem(z + d + nz, nz), y, lo, f)

    def at_y(d):
        return dev(z, lax.rem(y + d + ny, ny), lo, f)

    partners = [nxt, prv]
    if nz > 1:
        partners += [at_z(1), at_z(-1)]
    if ny > 1:
        partners += [at_y(1), at_y(-1)]
    partners += [row_dev(lax.rem(x8 + d, nx)) for d in range(1, nx)]
    barrier = pltpu.get_barrier_semaphore()
    for device in partners:
        pl.semaphore_signal(
            barrier, inc=1, device_id=device, device_id_type=pl.DeviceIdType.MESH
        )
    loads = [
        pltpu.make_async_copy(feat, fb, load_sem.at[0]),
        pltpu.make_async_copy(cot, cb, load_sem.at[1]),
        pltpu.make_async_copy(mast, wg.at[f], load_sem.at[2]),
    ]
    for copy in loads:
        copy.start()
    acc[...] = jnp.zeros_like(acc)
    pl.semaphore_wait(barrier, len(partners))

    def tell(step):
        reach = 1 << step
        for i, (n, at) in enumerate(((nz, at_z), (ny, at_y))):
            if reach < n // 2:
                for d in (reach, -reach):
                    pl.semaphore_signal(
                        near_sem.at[step, i], inc=1, device_id=at(d),
                        device_id_type=pl.DeviceIdType.MESH,
                    )

    def hear(step):
        reach = 1 << step
        for i, n in enumerate((nz, ny)):
            if reach < n // 2:
                pl.semaphore_wait(near_sem.at[step, i], 2)

    tell(0)

    kept = []
    beside = f + 1 - 2 * lax.rem(f, 2)
    across = lax.rem(f + 2, n_f)
    for d, target in ((1, beside), (2, across), (3, lax.rem(beside + 2, n_f))):
        copy = remote(mast, wg.at[f], filt_ss.at[d], filt_rs.at[f], (ctx, target))
        copy.start()
        kept.append(copy)
    halo_plan = [
        (feat.at[pl.ds(1, 2), pl.ds(length - 16, 16), :], hl_kv, nxt),
        (feat.at[0, pl.ds(length - 8, 8), :], hl_q, nxt),
        (cot.at[pl.ds(0, 8), :], hr_c, prv),
        (feat.at[0, pl.ds(0, 8), :], hr_q, prv),
        (cot.at[pl.ds(8, 8), :], lr_c, prv),
        (feat.at[0, pl.ds(8, 8), :], lr_q, prv),
        (feat.at[pl.ds(1, 2), pl.ds(0, 8), :], lr_kv, prv),
    ]
    halo = []
    for i, (src, dst, device) in enumerate(halo_plan):
        copy = remote(src, dst, halo_ss.at[i], halo_rs.at[i], device)
        if i < 4:
            copy.start()
        halo.append(copy)
    kept += halo

    for copy in loads:
        copy.wait()
    def hear_filters(src, i):
        remote(mast, wg.at[src], filt_ss.at[i], filt_rs.at[src], (ctx, src)).wait_recv()

    def place(tile, held):
        at = tile * LANE
        for j in range(TAPS):
            parts = []
            for i in held:
                low, high = max(at, i * portion), min(at + LANE, (i + 1) * portion)
                if low < high:
                    parts.append(wg[i, j, :, low - i * portion : high - i * portion])
            whole = jnp.concatenate(parts, axis=1)
            wv[tile, j] = whole.astype(BF16).astype(F32)

    pair = lax.div(f, 2)
    hear_filters(beside, 1)

    @pl.when(pair == 0)
    def _():
        place(0, (0, 1))

    @pl.when(pair == 1)
    def _():
        place(2, (2, 3))

    def taps(m, bank):
        return [wv[m, j, pl.ds(bank, 1), :] for j in range(TAPS)]

    def fir(ref, at, rows, w, sign):
        total = w[0] * ref[pl.ds(at, rows), :]
        for j in range(1, TAPS):
            total = total + w[j] * ref[pl.ds(at + sign * j, rows), :]
        return total

    def lanes_of(b):
        return pl.ds(pl.multiple_of(b * LANE, LANE), LANE)

    def q_rows(b, m, spans):
        w = taps(m, 0)
        for at, rows in spans:
            conv = fir(xq.at[b], 16 + at, rows, w, -1)
            qc[b, at : at + rows, :] = conv
            gm[b, at : at + rows, :] = conv * xc[b, at : at + rows, :]

    def kv_rows(b, m, spans):
        w = taps(m, 1)
        for at, rows in spans:
            kc[b, 8 + at : 8 + at + rows, :] = fir(xk.at[b], 16 + at, rows, w, -1)
        w = taps(m, 2)
        for at, rows in spans:
            own = slice(8 + at, 8 + at + rows)
            conv = fir(xv.at[b], 16 + at, rows, w, -1)
            vc[b, own, :] = conv
            pr[b, own, :] = conv * kc[b, own, :]

    def mixer_rows(b, m, spans, keep=True):
        w = taps(m, 3)
        for at, rows in spans:
            mixer = fir(pr.at[b], 8 + at, rows, w, -1)
            gq[b, at : at + rows, :] = mixer * xc[b, at : at + rows, :]
            if keep:
                mb[at : at + rows, lanes_of(b)] = (
                    mixer * qc[b, at : at + rows, :]
                ).astype(BF16)

    def product_rows(b, m, spans):
        w = taps(m, 3)
        for at, rows in spans:
            own = slice(8 + at, 8 + at + rows)
            grad = fir(gm.at[b], at, rows, w, 1)
            gk[b, at : at + rows, :] = grad * vc[b, own, :]
            gv[b, at : at + rows, :] = grad * kc[b, own, :]

    def filter_rows(b, m, bank, spans):
        grad = (gq, gk, gv, gm)[bank].at[b]
        source = (xq, xk, xv, pr)[bank].at[b]
        off = 8 if bank == 3 else 16
        sums = [None] * TAPS
        for at, rows in spans:
            g = grad[at : at + rows, :]
            for j in range(TAPS):
                part = g * source[pl.ds(off + at - j, rows), :]
                part = jnp.sum(part.reshape(rows // 8, 8, LANE), axis=0)
                sums[j] = part if sums[j] is None else sums[j] + part
        for j in range(TAPS):
            acc[m, 4 * j + bank] = acc[m, 4 * j + bank] + sums[j]

    def interior(b, carry):
        m = lax.rem(b, tiles)
        lanes = lanes_of(b)
        for ref, i in ((xq, 0), (xk, 1), (xv, 2)):
            ref[b, 16 : 16 + length, :] = fb[i, :, lanes].astype(F32)
        xc[b, 0:length, :] = cb[:, lanes].astype(F32)
        q_rows(b, m, chunks(8, length))
        kv_rows(b, m, chunks(8, length))
        mixer_rows(b, m, chunks(16, length))
        product_rows(b, m, chunks(8, length - 8))
        filter_rows(b, m, 0, chunks(16, length))
        filter_rows(b, m, 1, chunks(8, length - 8))
        filter_rows(b, m, 2, chunks(8, length - 8))
        filter_rows(b, m, 3, chunks(16, length))
        return carry

    own = 2 * pair

    def own_tile(i, carry):
        return interior(own + tiles * i, carry)

    def other_tiles(i, carry):
        m = jnp.where(lax.rem(i, 2) == 0, 1, 2 - own)
        return interior(m + tiles * lax.div(i, 2), carry)

    lax.fori_loop(0, blocks // tiles, own_tile, 0)
    for i in range(2):
        hear_filters(2 - own + i, 2 + i)
    hear(0)
    tell(1)

    @pl.when(pair == 0)
    def _():
        place(1, range(n_f))
        place(2, range(n_f))

    @pl.when(pair == 1)
    def _():
        place(0, range(n_f))
        place(1, range(n_f))

    lax.fori_loop(0, blocks - blocks // tiles, other_tiles, 0)
    for copy in halo[4:]:
        copy.start()
    hear(1)
    tell(2)
    for copy in halo[:4]:
        copy.wait_recv()

    def edge(ref, lanes, drop):
        return jnp.where(drop, 0.0, ref[:, lanes].astype(F32))

    def edges(b, carry):
        m = lax.rem(b, tiles)
        lanes = lanes_of(b)
        xq[b, 8:16, :] = edge(hl_q, lanes, first)
        xk[b, 0:16, :] = edge(hl_kv.at[0], lanes, first)
        xv[b, 0:16, :] = edge(hl_kv.at[1], lanes, first)
        xc[b, length : length + 8, :] = edge(hr_c, lanes, last)
        xq[b, 16 + length : 24 + length, :] = edge(hr_q, lanes, last)
        ends = [(0, 8), (length - 8, 8)]
        q_rows(b, m, [(0, 8), (length, 8)])
        kv_rows(b, m, [(-8, 16)])
        mixer_rows(b, m, [(0, 16)])
        product_rows(b, m, ends)
        filter_rows(b, m, 0, [(0, 16)])
        filter_rows(b, m, 1, ends)
        filter_rows(b, m, 2, ends)
        filter_rows(b, m, 3, [(0, 16)])
        return carry

    lax.fori_loop(0, blocks, edges, 0)
    out_mixed = pltpu.make_async_copy(mb, mixed_o, out_sem.at[0])
    out_mixed.start()

    lane_at = lax.broadcasted_iota(jnp.int32, (8, LANE), 1)
    for pair in range(4):
        parts = [
            jnp.sum(acc[m, 8 * pair : 8 * pair + 8], axis=1) for m in range(tiles)
        ]
        for g in range(n_f):
            m, off = divmod(g * portion, LANE)
            piece = pltpu.roll(parts[m], (LANE - off) % LANE, 1) if off else parts[m]
            if off + portion > LANE:
                rest = pltpu.roll(parts[m + 1], LANE - off, 1)
                piece = jnp.where(lane_at < LANE - off, piece, rest)
            for i in range(2):
                half, tap = divmod(2 * pair + i, 4)
                s1s[g * LO + half, tap] = piece[4 * i : 4 * i + 4]
    for d in range(1, nx):
        s = lax.rem(x8 + d, nx)
        copy = remote(s1s.at[s], s1r.at[x8], s1_ss.at[d], s1_rs.at[x8], row_dev(s))
        copy.start()
        kept.append(copy)
    s1r[x8] = s1s[x8]
    for d in range(1, nx):
        s = lax.rem(x8 + d, nx)
        remote(s1s.at[s], s1r.at[s], s1_ss.at[d], s1_rs.at[s], row_dev(s)).wait_recv()
    total = s1r[0]
    for s in range(1, nx):
        total = total + s1r[s]
    s2s[...] = total

    mine = lax.rem(y, 4)
    for d in far_first(ny):
        s = lax.rem(y + d, ny)
        copy = remote(
            s2s.at[lax.rem(s, 4)], s2r.at[y], s2_ss.at[d], s2_rs.at[y], dev(z, s, lo, f)
        )
        copy.start()
        kept.append(copy)
    s2r[y] = s2s[mine]
    for d in range(1, ny):
        s = lax.rem(y + d, ny)
        remote(
            s2s.at[mine], s2r.at[s], s2_ss.at[d], s2_rs.at[s], dev(z, s, lo, f)
        ).wait_recv()
    total = s2r[0]
    for s in range(1, ny):
        total = total + s2r[s]
    s3s[...] = total

    hear(2)
    for d in far_first(nz):
        s = lax.rem(z + d, nz)
        copy = remote(s3s, s3r.at[z], s3_ss.at[d], s3_rs.at[z], dev(s, y, lo, f))
        copy.start()
        kept.append(copy)
    s3r[z] = s3s[...]

    for copy in halo[4:]:
        copy.wait_recv()

    def second_pass(b, carry):
        m = lax.rem(b, tiles)
        lanes = lanes_of(b)
        xc[b, length + 8 : length + 16, :] = edge(lr_c, lanes, last)
        xq[b, 24 + length : 32 + length, :] = edge(lr_q, lanes, last)
        xk[b, 16 + length : 24 + length, :] = edge(lr_kv.at[0], lanes, last)
        xv[b, 16 + length : 24 + length, :] = edge(lr_kv.at[1], lanes, last)
        past = [(length, 8)]
        q_rows(b, m, [(length + 8, 8)])
        kv_rows(b, m, past)
        mixer_rows(b, m, past, keep=False)
        product_rows(b, m, past)
        for bank, grad in enumerate((gq.at[b], gk.at[b], gv.at[b])):
            w = taps(m, bank)
            for at, rows in chunks(0, length):
                gb[bank, at : at + rows, lanes] = fir(grad, at, rows, w, 1).astype(BF16)
        return carry

    lax.fori_loop(0, blocks, second_pass, 0)
    out_grads = pltpu.make_async_copy(gb, grads_o, out_sem.at[1])
    out_grads.start()

    for d in range(1, nz):
        s = lax.rem(z + d, nz)
        remote(s3s, s3r.at[s], s3_ss.at[d], s3_rs.at[s], dev(s, y, lo, f)).wait_recv()
    total = s3r[0]
    for s in range(1, nz):
        total = total + s3r[s]
    s4s[...] = total

    tap = lo * 4 + mine
    for i, (d, other) in enumerate(
        ((2, 1), (2, 0), (-1, 1), (1, 1), (-1, 0), (1, 0), (0, 1))
    ):
        device = dev(z, lax.rem(y + d + ny, ny), 1 - lo if other else lo, f)
        copy = remote(s4s, res.at[tap], s4_ss.at[i], s4_rs.at[tap], device)
        copy.start()
        kept.append(copy)
    out_res = pltpu.make_async_copy(s4s, res.at[tap], out_sem.at[2])
    out_res.start()
    for d in range(1, LO * 4):
        s = lax.rem(tap + d, LO * 4)
        remote(s4s, res.at[s], s4_ss.at[0], s4_rs.at[s], nxt).wait_recv()

    for copy in kept:
        copy.wait_send()
    out_mixed.wait()
    out_grads.wait()
    out_res.wait()


def write(factor, mixed, grads, res, mixed_o, grads_o, filt_o, big, small, done, sem):
    pieces = [(res, small)] + [(mixed, big.at[3])]
    pieces += [(grads.at[i], big.at[i]) for i in range(3)]
    reads = [
        pltpu.make_async_copy(src, dst, sem.at[0, i])
        for i, (src, dst) in enumerate(pieces)
    ]
    for copy in reads:
        copy.start()
    reads[0].wait()
    portion = filt_o.shape[2]
    for j in range(TAPS):
        done[j] = small[j][:, :portion] * factor
    outs = [(done, filt_o), (big.at[3], mixed_o)]
    outs += [(big.at[i], grads_o.at[i]) for i in range(3)]
    writes = [
        pltpu.make_async_copy(src, dst, sem.at[1, i])
        for i, (src, dst) in enumerate(outs)
    ]
    writes[0].start()
    for i in range(1, 5):
        reads[i].wait()
        writes[i].start()
    for copy in writes:
        copy.wait()


def per_device(n_ctx, n_f, ny, features, cotangent, master_filters):
    _, length, width = features.shape
    portion = master_filters.shape[2]
    groups = portion * n_f
    repeats = width // groups
    count_all = length * n_ctx * repeats * n_f
    factor = 1.0 / math.sqrt(count_all)
    nz = n_ctx // (LO * ny)
    nx = n_f * LO
    blocks = width // LANE
    tiles = groups // LANE
    vm = pltpu.VMEM
    dma = pltpu.SemaphoreType.DMA
    scratch = [
        vm((3, length, width), BF16), vm((length, width), BF16),
        vm((length, width), BF16), vm((3, length, width), BF16),
        vm((8, width), BF16), vm((2, 16, width), BF16),
        vm((8, width), BF16), vm((8, width), BF16),
        vm((8, width), BF16), vm((8, width), BF16), vm((2, 8, width), BF16),
        vm((n_f, TAPS, 4, portion), F32), vm((tiles, TAPS, 4, LANE), F32),
    ]
    scratch += [vm((blocks, length + 32, LANE), F32)] * 3
    scratch += [vm((blocks, length + 16, LANE), F32)] * 6
    scratch += [vm((blocks, length + 8, LANE), F32)] * 3
    scratch += [
        vm((tiles, 32, 8, LANE), F32),
        vm((nx, 4, 4, LANE), F32), vm((nx, 4, 4, LANE), F32),
        vm((4, 4, LANE), F32), vm((ny, 4, LANE), F32),
        vm((4, LANE), F32), vm((nz, 4, LANE), F32), vm((4, LANE), F32),
        dma((3,)), dma((7,)), dma((7,)), dma((n_f,)), dma((n_f,)),
        dma((nx,)), dma((nx,)), dma((ny,)), dma((ny,)), dma((nz,)), dma((nz,)),
        dma((7,)), dma((8,)), dma((3,)), pltpu.SemaphoreType.REGULAR((3, 2)),
    ]
    anywhere = pl.BlockSpec(memory_space=pl.ANY)
    big = (
        jax.ShapeDtypeStruct((length, width), BF16),
        jax.ShapeDtypeStruct((3, length, width), BF16),
    )
    mixed, grads, res = pl.pallas_call(
        functools.partial(kernel, n_ctx, n_f, ny),
        out_shape=big + (jax.ShapeDtypeStruct((8, 4, LANE), F32),),
        in_specs=[anywhere] * 3,
        out_specs=(anywhere,) * 3,
        scratch_shapes=scratch,
        compiler_params=pltpu.CompilerParams(
            collective_id=0, has_side_effects=True, vmem_limit_bytes=ALL_VMEM
        ),
    )(features, cotangent, jnp.transpose(master_filters, (1, 0, 2)))
    mixed, grads, filters = pl.pallas_call(
        functools.partial(write, factor),
        out_shape=big + (jax.ShapeDtypeStruct((TAPS, 4, portion), F32),),
        in_specs=[anywhere] * 3,
        out_specs=(anywhere,) * 3,
        scratch_shapes=[
            vm((4, length, width), BF16), vm((8, 4, LANE), F32),
            vm((TAPS, 4, portion), F32), dma((2, 5)),
        ],
        compiler_params=pltpu.CompilerParams(vmem_limit_bytes=ALL_VMEM),
    )(mixed, grads, res)
    return mixed, grads, jnp.transpose(filters, (1, 0, 2))


def solution(mesh, ny=NY):
    return jax.shard_map(
        functools.partial(per_device, mesh.shape["ctx"], mesh.shape["fsdp"], ny),
        mesh=mesh,
        in_specs=(P(None, "ctx", "fsdp"), P("ctx", "fsdp"), P(None, None, "fsdp")),
        out_specs=(P("ctx", "fsdp"), P(None, "ctx", "fsdp"), P(None, None, "fsdp")),
        check_vma=False,
    )
```

```python
import functools
import math

import jax
import jax.numpy as jnp
from jax import lax
from jax.experimental import pallas as pl
from jax.experimental.pallas import tpu as pltpu
from jax.sharding import PartitionSpec as P

LO = 2
NY = 8
TAPS = 7
LANE = 128
F32 = jnp.float32
BF16 = jnp.bfloat16
ALL_VMEM = 67043328


def chunks(first, end, most=64):
    return [(at, min(most, end - at)) for at in range(first, end, most)]


def far_first(n):
    return sorted(range(1, n), key=lambda d: -min(d, n - d))


def kernel(
    n_ctx, n_f, ny,
    feat, cot, mast,
    mixed_o, grads_o, res,
    fb, cb, mb, gb, hl_q, hl_kv, hr_c, hr_q, lr_c, lr_q, lr_kv, wg, wv,
    xq, xk, xv, xc, qc, kc, vc, pr, gm, gq, gk, gv, acc,
    s1s, s1r, s3s, s3r, s4s,
    load_sem, halo_ss, halo_rs, filt_ss, filt_rs,
    s1_ss, s1_rs, s3_ss, s3_rs, s4_ss, s4_rs, out_sem, near_sem,
):
    length = fb.shape[1]
    blocks = fb.shape[2] // LANE
    portion = mast.shape[2]
    tiles = wv.shape[0]
    nz = n_ctx // (LO * ny)
    nx = n_f * LO
    ctx = lax.axis_index("ctx")
    f = lax.axis_index("fsdp")
    lo = lax.rem(ctx, LO)
    y = lax.rem(lax.div(ctx, LO), ny)
    z = lax.div(ctx, LO * ny)
    x8 = f * LO + lo
    first = ctx == 0
    last = ctx == n_ctx - 1

    def dev(z_, y_, lo_, f_):
        return ((z_ * ny + y_) * LO + lo_, f_)

    def row_dev(s):
        return dev(z, y, lax.rem(s, LO), lax.div(s, LO))

    nxt = (lax.rem(ctx + 1, n_ctx), f)
    prv = (lax.rem(ctx + n_ctx - 1, n_ctx), f)

    def remote(src, dst, ss, rs, device):
        return pltpu.make_async_remote_copy(
            src_ref=src, dst_ref=dst, send_sem=ss, recv_sem=rs,
            device_id=device, device_id_type=pl.DeviceIdType.MESH,
        )

    def at_z(d):
        return dev(lax.rem(z + d + nz, nz), y, lo, f)

    def at_y(d):
        return dev(z, lax.rem(y + d + ny, ny), lo, f)

    partners = [nxt, prv]
    if nz > 1:
        partners += [at_z(1), at_z(-1)]
    if ny > 1:
        partners += [at_y(1), at_y(-1), at_y(2), at_y(-2)]
    partners += [row_dev(lax.rem(x8 + d, nx)) for d in range(1, nx)]
    barrier = pltpu.get_barrier_semaphore()
    for device in partners:
        pl.semaphore_signal(
            barrier, inc=1, device_id=device, device_id_type=pl.DeviceIdType.MESH
        )
    loads = [
        pltpu.make_async_copy(feat, fb, load_sem.at[0]),
        pltpu.make_async_copy(cot, cb, load_sem.at[1]),
        pltpu.make_async_copy(mast, wg.at[f], load_sem.at[2]),
    ]
    for copy in loads:
        copy.start()
    acc[...] = jnp.zeros_like(acc)
    pl.semaphore_wait(barrier, len(partners))

    steps_z = [r for r in (1, 2, 4) if r < nz // 2]
    signals = [
        [at_z(d) for r in steps_z[i : i + 1] for d in (r, -r)] for i in range(3)
    ]
    signals[0] += [at_y(d) for d in (1, -1, 2, -2)]
    signals[1] += [at_y(d) for d in (2, -2)]

    def tell(step):
        for device in signals[step]:
            pl.semaphore_signal(
                near_sem.at[step], inc=1, device_id=device,
                device_id_type=pl.DeviceIdType.MESH,
            )

    def hear(step):
        if signals[step]:
            pl.semaphore_wait(near_sem.at[step], len(signals[step]))

    tell(0)

    kept = []
    beside = f + 1 - 2 * lax.rem(f, 2)
    across = lax.rem(f + 2, n_f)
    for d, target in ((1, beside), (2, across), (3, lax.rem(beside + 2, n_f))):
        copy = remote(mast, wg.at[f], filt_ss.at[d], filt_rs.at[f], (ctx, target))
        copy.start()
        kept.append(copy)
    halo_plan = [
        (feat.at[pl.ds(1, 2), pl.ds(length - 16, 16), :], hl_kv, nxt),
        (feat.at[0, pl.ds(length - 8, 8), :], hl_q, nxt),
        (cot.at[pl.ds(0, 8), :], hr_c, prv),
        (feat.at[0, pl.ds(0, 8), :], hr_q, prv),
        (cot.at[pl.ds(8, 8), :], lr_c, prv),
        (feat.at[0, pl.ds(8, 8), :], lr_q, prv),
        (feat.at[pl.ds(1, 2), pl.ds(0, 8), :], lr_kv, prv),
    ]
    halo = []
    for i, (src, dst, device) in enumerate(halo_plan):
        copy = remote(src, dst, halo_ss.at[i], halo_rs.at[i], device)
        if i < 4:
            copy.start()
        halo.append(copy)
    kept += halo

    for copy in loads:
        copy.wait()
    def hear_filters(src, i):
        remote(mast, wg.at[src], filt_ss.at[i], filt_rs.at[src], (ctx, src)).wait_recv()

    def place(tile, held):
        at = tile * LANE
        for j in range(TAPS):
            parts = []
            for i in held:
                low, high = max(at, i * portion), min(at + LANE, (i + 1) * portion)
                if low < high:
                    parts.append(wg[i, j, :, low - i * portion : high - i * portion])
            whole = jnp.concatenate(parts, axis=1)
            wv[tile, j] = whole.astype(BF16).astype(F32)

    pair = lax.div(f, 2)
    hear_filters(beside, 1)

    @pl.when(pair == 0)
    def _():
        place(0, (0, 1))

    @pl.when(pair == 1)
    def _():
        place(2, (2, 3))

    def taps(m, bank):
        return [wv[m, j, pl.ds(bank, 1), :] for j in range(TAPS)]

    def fir(ref, at, rows, w, sign):
        total = w[0] * ref[pl.ds(at, rows), :]
        for j in range(1, TAPS):
            total = total + w[j] * ref[pl.ds(at + sign * j, rows), :]
        return total

    def lanes_of(b):
        return pl.ds(pl.multiple_of(b * LANE, LANE), LANE)

    def q_rows(b, m, spans):
        w = taps(m, 0)
        for at, rows in spans:
            conv = fir(xq.at[b], 16 + at, rows, w, -1)
            qc[b, at : at + rows, :] = conv
            gm[b, at : at + rows, :] = conv * xc[b, at : at + rows, :]

    def kv_rows(b, m, spans):
        w = taps(m, 1)
        for at, rows in spans:
            kc[b, 8 + at : 8 + at + rows, :] = fir(xk.at[b], 16 + at, rows, w, -1)
        w = taps(m, 2)
        for at, rows in spans:
            own = slice(8 + at, 8 + at + rows)
            conv = fir(xv.at[b], 16 + at, rows, w, -1)
            vc[b, own, :] = conv
            pr[b, own, :] = conv * kc[b, own, :]

    def mixer_rows(b, m, spans, keep=True):
        w = taps(m, 3)
        for at, rows in spans:
            mixer = fir(pr.at[b], 8 + at, rows, w, -1)
            gq[b, at : at + rows, :] = mixer * xc[b, at : at + rows, :]
            if keep:
                mb[at : at + rows, lanes_of(b)] = (
                    mixer * qc[b, at : at + rows, :]
                ).astype(BF16)

    def product_rows(b, m, spans):
        w = taps(m, 3)
        for at, rows in spans:
            own = slice(8 + at, 8 + at + rows)
            grad = fir(gm.at[b], at, rows, w, 1)
            gk[b, at : at + rows, :] = grad * vc[b, own, :]
            gv[b, at : at + rows, :] = grad * kc[b, own, :]

    def filter_rows(b, m, bank, spans):
        grad = (gq, gk, gv, gm)[bank].at[b]
        source = (xq, xk, xv, pr)[bank].at[b]
        off = 8 if bank == 3 else 16
        sums = [None] * TAPS
        for at, rows in spans:
            g = grad[at : at + rows, :]
            for j in range(TAPS):
                part = g * source[pl.ds(off + at - j, rows), :]
                part = jnp.sum(part.reshape(rows // 8, 8, LANE), axis=0)
                sums[j] = part if sums[j] is None else sums[j] + part
        for j in range(TAPS):
            acc[m, 4 * j + bank] = acc[m, 4 * j + bank] + sums[j]

    def interior(b, carry):
        m = lax.rem(b, tiles)
        lanes = lanes_of(b)
        for ref, i in ((xq, 0), (xk, 1), (xv, 2)):
            ref[b, 16 : 16 + length, :] = fb[i, :, lanes].astype(F32)
        xc[b, 0:length, :] = cb[:, lanes].astype(F32)
        q_rows(b, m, chunks(8, length))
        kv_rows(b, m, chunks(8, length))
        mixer_rows(b, m, chunks(16, length))
        product_rows(b, m, chunks(8, length - 8))
        filter_rows(b, m, 0, chunks(16, length))
        filter_rows(b, m, 1, chunks(8, length - 8))
        filter_rows(b, m, 2, chunks(8, length - 8))
        filter_rows(b, m, 3, chunks(16, length))
        return carry

    own = 2 * pair

    def own_tile(i, carry):
        return interior(own + tiles * i, carry)

    def other_tiles(i, carry):
        m = jnp.where(lax.rem(i, 2) == 0, 1, 2 - own)
        return interior(m + tiles * lax.div(i, 2), carry)

    lax.fori_loop(0, blocks // tiles, own_tile, 0)
    for i in range(2):
        hear_filters(2 - own + i, 2 + i)
    hear(0)
    tell(1)

    @pl.when(pair == 0)
    def _():
        place(1, range(n_f))
        place(2, range(n_f))

    @pl.when(pair == 1)
    def _():
        place(0, range(n_f))
        place(1, range(n_f))

    lax.fori_loop(0, blocks - blocks // tiles, other_tiles, 0)
    for copy in halo[4:]:
        copy.start()
    hear(1)
    tell(2)
    for copy in halo[:4]:
        copy.wait_recv()

    def edge(ref, lanes, drop):
        return jnp.where(drop, 0.0, ref[:, lanes].astype(F32))

    def edges(b, carry):
        m = lax.rem(b, tiles)
        lanes = lanes_of(b)
        xq[b, 8:16, :] = edge(hl_q, lanes, first)
        xk[b, 0:16, :] = edge(hl_kv.at[0], lanes, first)
        xv[b, 0:16, :] = edge(hl_kv.at[1], lanes, first)
        xc[b, length : length + 8, :] = edge(hr_c, lanes, last)
        xq[b, 16 + length : 24 + length, :] = edge(hr_q, lanes, last)
        ends = [(0, 8), (length - 8, 8)]
        q_rows(b, m, [(0, 8), (length, 8)])
        kv_rows(b, m, [(-8, 16)])
        mixer_rows(b, m, [(0, 16)])
        product_rows(b, m, ends)
        filter_rows(b, m, 0, [(0, 16)])
        filter_rows(b, m, 1, ends)
        filter_rows(b, m, 2, ends)
        filter_rows(b, m, 3, [(0, 16)])
        return carry

    lax.fori_loop(0, blocks, edges, 0)
    out_mixed = pltpu.make_async_copy(mb, mixed_o, out_sem.at[0])
    out_mixed.start()

    lane_at = lax.broadcasted_iota(jnp.int32, (8, LANE), 1)
    for pair in range(4):
        parts = [
            jnp.sum(acc[m, 8 * pair : 8 * pair + 8], axis=1) for m in range(tiles)
        ]
        for g in range(n_f):
            m, off = divmod(g * portion, LANE)
            piece = pltpu.roll(parts[m], (LANE - off) % LANE, 1) if off else parts[m]
            if off + portion > LANE:
                rest = pltpu.roll(parts[m + 1], LANE - off, 1)
                piece = jnp.where(lane_at < LANE - off, piece, rest)
            for i in range(2):
                half, tap = divmod(2 * pair + i, 4)
                s1s[g * LO + half, tap] = piece[4 * i : 4 * i + 4]
    mine = lax.rem(y, 4)
    for d in far_first(ny) + [0]:
        y_ = lax.rem(y + d, ny)
        for e in range(nx) if d else range(1, nx):
            s = lax.rem(x8 + e, nx)
            remote(
                s1s.at[s, lax.rem(y_, 4)], s1r.at[y * nx + x8], s1_ss.at[0], s1_rs.at[0],
                dev(z, y_, lax.rem(s, LO), lax.div(s, LO)),
            ).start()
    s1r[y * nx + x8] = s1s[x8, mine]
    others = s1r.at[pl.ds(0, ny * nx - 1)]
    every = remote(others, others, s1_ss.at[0], s1_rs.at[0], nxt)
    every.wait_recv()
    sums = [s1r[i] for i in range(ny * nx)]
    while len(sums) > 1:
        sums = [a + b for a, b in zip(sums[::2], sums[1::2], strict=True)]
    s3s[...] = sums[0]

    hear(2)
    for d in range(1, nz):
        s = jnp.where(d <= z, d - 1, d)
        copy = remote(s3s, s3r.at[z], s3_ss.at[d], s3_rs.at[z], dev(s, y, lo, f))
        copy.start()
        kept.append(copy)
    s3r[z] = s3s[...]

    for copy in halo[4:]:
        copy.wait_recv()

    def second_pass(b, carry):
        m = lax.rem(b, tiles)
        lanes = lanes_of(b)
        xc[b, length + 8 : length + 16, :] = edge(lr_c, lanes, last)
        xq[b, 24 + length : 32 + length, :] = edge(lr_q, lanes, last)
        xk[b, 16 + length : 24 + length, :] = edge(lr_kv.at[0], lanes, last)
        xv[b, 16 + length : 24 + length, :] = edge(lr_kv.at[1], lanes, last)
        past = [(length, 8)]
        q_rows(b, m, [(length + 8, 8)])
        kv_rows(b, m, past)
        mixer_rows(b, m, past, keep=False)
        product_rows(b, m, past)
        for bank, grad in enumerate((gq.at[b], gk.at[b], gv.at[b])):
            w = taps(m, bank)
            for at, rows in chunks(0, length):
                gb[bank, at : at + rows, lanes] = fir(grad, at, rows, w, 1).astype(BF16)
        return carry

    lax.fori_loop(0, blocks, second_pass, 0)
    out_grads = pltpu.make_async_copy(gb, grads_o, out_sem.at[1])
    out_grads.start()

    for d in range(1, nz):
        s = lax.rem(z + d, nz)
        remote(s3s, s3r.at[s], s3_ss.at[d], s3_rs.at[s], dev(s, y, lo, f)).wait_recv()
    total = s3r[0]
    for s in range(1, nz):
        total = total + s3r[s]
    s4s[...] = total

    tap = lo * 4 + mine
    for i, (d, other) in enumerate(
        ((2, 1), (2, 0), (-1, 1), (1, 1), (-1, 0), (1, 0), (0, 1))
    ):
        device = dev(z, lax.rem(y + d + ny, ny), 1 - lo if other else lo, f)
        copy = remote(s4s, res.at[tap], s4_ss.at[i], s4_rs.at[tap], device)
        copy.start()
        kept.append(copy)
    out_res = pltpu.make_async_copy(s4s, res.at[tap], out_sem.at[2])
    out_res.start()
    for d in range(1, LO * 4):
        s = lax.rem(tap + d, LO * 4)
        remote(s4s, res.at[s], s4_ss.at[0], s4_rs.at[s], nxt).wait_recv()

    for copy in kept:
        copy.wait_send()
    every.wait_send()
    out_mixed.wait()
    out_grads.wait()
    out_res.wait()


def write(factor, mixed, grads, res, mixed_o, grads_o, filt_o, big, small, done, sem):
    pieces = [(res, small)] + [(mixed, big.at[3])]
    pieces += [(grads.at[i], big.at[i]) for i in range(3)]
    reads = [
        pltpu.make_async_copy(src, dst, sem.at[0, i])
        for i, (src, dst) in enumerate(pieces)
    ]
    for copy in reads:
        copy.start()
    reads[0].wait()
    portion = filt_o.shape[2]
    for j in range(TAPS):
        done[j] = small[j][:, :portion] * factor
    outs = [(done, filt_o), (big.at[3], mixed_o)]
    outs += [(big.at[i], grads_o.at[i]) for i in range(3)]
    writes = [
        pltpu.make_async_copy(src, dst, sem.at[1, i])
        for i, (src, dst) in enumerate(outs)
    ]
    writes[0].start()
    for i in range(1, 5):
        reads[i].wait()
        writes[i].start()
    for copy in writes:
        copy.wait()


def per_device(n_ctx, n_f, ny, features, cotangent, master_filters):
    _, length, width = features.shape
    portion = master_filters.shape[2]
    groups = portion * n_f
    repeats = width // groups
    count_all = length * n_ctx * repeats * n_f
    factor = 1.0 / math.sqrt(count_all)
    nz = n_ctx // (LO * ny)
    nx = n_f * LO
    blocks = width // LANE
    tiles = groups // LANE
    vm = pltpu.VMEM
    dma = pltpu.SemaphoreType.DMA
    scratch = [
        vm((3, length, width), BF16), vm((length, width), BF16),
        vm((length, width), BF16), vm((3, length, width), BF16),
        vm((8, width), BF16), vm((2, 16, width), BF16),
        vm((8, width), BF16), vm((8, width), BF16),
        vm((8, width), BF16), vm((8, width), BF16), vm((2, 8, width), BF16),
        vm((n_f, TAPS, 4, portion), F32), vm((tiles, TAPS, 4, LANE), F32),
    ]
    scratch += [vm((blocks, length + 32, LANE), F32)] * 3
    scratch += [vm((blocks, length + 16, LANE), F32)] * 6
    scratch += [vm((blocks, length + 8, LANE), F32)] * 3
    scratch += [
        vm((tiles, 32, 8, LANE), F32),
        vm((nx, 4, 4, LANE), F32), vm((ny * nx, 4, LANE), F32),
        vm((4, LANE), F32), vm((nz, 4, LANE), F32), vm((4, LANE), F32),
        dma((3,)), dma((7,)), dma((7,)), dma((n_f,)), dma((n_f,)),
        dma((1,)), dma((1,)), dma((nz,)), dma((nz,)),
        dma((7,)), dma((8,)), dma((3,)), pltpu.SemaphoreType.REGULAR((3,)),
    ]
    anywhere = pl.BlockSpec(memory_space=pl.ANY)
    big = (
        jax.ShapeDtypeStruct((length, width), BF16),
        jax.ShapeDtypeStruct((3, length, width), BF16),
    )
    mixed, grads, res = pl.pallas_call(
        functools.partial(kernel, n_ctx, n_f, ny),
        out_shape=big + (jax.ShapeDtypeStruct((8, 4, LANE), F32),),
        in_specs=[anywhere] * 3,
        out_specs=(anywhere,) * 3,
        scratch_shapes=scratch,
        compiler_params=pltpu.CompilerParams(
            collective_id=0, has_side_effects=True, vmem_limit_bytes=ALL_VMEM
        ),
    )(features, cotangent, jnp.transpose(master_filters, (1, 0, 2)))
    mixed, grads, filters = pl.pallas_call(
        functools.partial(write, factor),
        out_shape=big + (jax.ShapeDtypeStruct((TAPS, 4, portion), F32),),
        in_specs=[anywhere] * 3,
        out_specs=(anywhere,) * 3,
        scratch_shapes=[
            vm((4, length, width), BF16), vm((8, 4, LANE), F32),
            vm((TAPS, 4, portion), F32), dma((2, 5)),
        ],
        compiler_params=pltpu.CompilerParams(vmem_limit_bytes=ALL_VMEM),
    )(mixed, grads, res)
    return mixed, grads, jnp.transpose(filters, (1, 0, 2))


def solution(mesh, ny=NY):
    return jax.shard_map(
        functools.partial(per_device, mesh.shape["ctx"], mesh.shape["fsdp"], ny),
        mesh=mesh,
        in_specs=(P(None, "ctx", "fsdp"), P("ctx", "fsdp"), P(None, None, "fsdp")),
        out_specs=(P("ctx", "fsdp"), P(None, "ctx", "fsdp"), P(None, None, "fsdp")),
        check_vma=False,
    )
```
